256 devices in a mesh: rows: 16 (over x_hi, y, core), modes: 16 (over x_lo, z).
Axes of the slice: x: 4 (x_hi: 2, x_lo: 2; x = x_hi * 2 + x_lo), y: 4, z: 8, core: 2. Of those that a mesh axis runs over, the one named last changes fastest.
Arguments:
- transfer: float32 [16384, 16384], P('rows', 'modes'), may hold values from -1 to 1
- observed: float32 [256, 16384], P('modes', 'rows'), may hold values from -6 to 6
- start: float32 [256, 16384], P('rows', 'modes'), may hold values from -6 to 6
- probe: bfloat16 [256, 16384], P(('rows', 'modes')), may hold values from -6 to 6
- w_first: bfloat16 [9, 48, 2], replicated, may hold values from -1.5 to 1.5
- w_mid: bfloat16 [9, 48, 48], replicated, may hold values from -0.3125 to 0.3125
- w_last: bfloat16 [9, 1, 48], replicated, may hold values from -0.3125 to 0.3125
Outputs:
- recovered: float32 [256, 16384], P(('rows', 'modes'))
The draws below stay inside these ranges and needn't reach their ends.
All inputs are finite; a program needn't handle non-finite values.
Results may differ from the reference program's by a relative error of at most 0.0049.
Values sent between devices are 32-bit elements; how exact they have to be, the bound alone decides.
No kernel may reach another device: no remote copies, remote signals or barrier semaphores. Data moves between devices by JAX's collectives and lax.ppermute only.
A program may use at most 128 MiB of HBM per device.

```python
import jax
import jax.numpy as jnp
from jax import lax

DET = 16384
IMG = 128
CH = 48
ITERS = 2
PIX = 16384
FRAMES = 256


def draw_transfer(key, part):
    key_entries, key_rows, key_cols = jax.random.split(key, 3)
    row_pos = jnp.arange(DET, dtype=jnp.float32) / DET
    col_pos = jnp.arange(PIX, dtype=jnp.float32) / PIX
    raw_entries = jnp.clip(jax.random.normal(key_entries, (DET, PIX), jnp.float32), -4.0, 4.0)
    row_scale = jnp.exp(jax.random.uniform(key_rows, (DET,), jnp.float32, -1.151, 1.151))
    col_scale = jnp.exp(jax.random.uniform(key_cols, (PIX,), jnp.float32, -1.151, 1.151))
    row_scale = row_scale * jnp.sqrt(1.0 + 2.0 * row_pos)
    col_scale = col_scale * jnp.sqrt(1.0 + 2.0 * col_pos)
    return raw_entries * row_scale[:, None] * col_scale[None, :] / IMG


def shard_levels(own_key, shape, pieces, low, top_value):
    level, own = 1.0, jax.random.fold_in(own_key, 6)
    for dim, parts in pieces:
        steps = jnp.exp(jax.random.uniform(jax.random.fold_in(own, dim), (parts,), jnp.float32, low / len(pieces), top_value / len(pieces)))
        level = level * jnp.repeat(steps, shape[dim] // parts).reshape([-1 if axis == dim else 1 for axis in range(len(shape))])
    return level


def noise(key, shape, width, limit, cuts=(), kind=jnp.bfloat16):
    factor_of = shard_levels(key, shape, cuts, -0.22, 0.18) if cuts else 1.0
    values = jax.random.normal(key, shape, jnp.float32) * width * factor_of
    return jnp.minimum(jnp.maximum(values, -limit), limit).astype(kind)


def setup_inputs(seed: int = 0) -> dict:
    streams_of = jax.random.split(jax.random.key(seed), 8)
    return {
        "transfer": draw_transfer(jax.random.fold_in(streams_of[7], 71), 0),
        "observed": noise(streams_of[1], (FRAMES, DET), 1.0, 6.0, ((0, 16), (1, 16)), jnp.float32),
        "start": noise(streams_of[2], (FRAMES, PIX), 1.0, 6.0, ((0, 16), (1, 16)), jnp.float32),
        "probe": noise(streams_of[3], (FRAMES, PIX), 1.0, 6.0, ((0, 256),)),
        "w_first": noise(streams_of[4], (9, CH, 2), 18 ** -0.5, 1.5),
        "w_mid": noise(streams_of[5], (9, CH, CH), (9 * CH) ** -0.5, 0.3125),
        "w_last": noise(streams_of[6], (9, 1, CH), (9 * CH) ** -0.5, 0.3125),
    }


def conv_layer(weights, feature):
    extent_rows, extent_cols = (feature.shape[1], feature.shape[2])
    padded = jnp.pad(feature.astype(jnp.float32), ((0, 0), (1, 1), (1, 1)))
    summed = jnp.zeros((weights.shape[1], extent_rows, extent_cols), jnp.float32)
    for offset in range(9):
        row_shift = offset // 3
        col_shift = offset % 3
        window = padded[:, row_shift:row_shift + extent_rows, col_shift:col_shift + extent_cols]
        summed = summed + jnp.einsum('oc,chw->ohw', weights[offset].astype(jnp.float32), window, precision=lax.Precision.HIGHEST)
    return summed

def silu_slope(values):
    logistic = jax.nn.sigmoid(values)
    return logistic * (1.0 + values * (1.0 - logistic))

def denoise(bundle, w_first, w_mid, w_last):
    pushed_one, levels_one, probe_one = bundle
    picture = pushed_one.reshape(IMG, IMG)
    stacked = jnp.stack([picture, jnp.zeros_like(picture) + levels_one]).astype(jnp.bfloat16)
    first_pre = conv_layer(w_first, stacked)
    first_tan = conv_layer(w_first[:, :, 0:1], probe_one.reshape(1, IMG, IMG))
    active_one = jax.nn.silu(first_pre).astype(jnp.bfloat16)
    tan_one = (silu_slope(first_pre) * first_tan).astype(jnp.bfloat16)
    second_pre = conv_layer(w_mid, active_one)
    second_tan = conv_layer(w_mid, tan_one)
    active_two = jax.nn.silu(second_pre).astype(jnp.bfloat16)
    tan_two = (silu_slope(second_pre) * second_tan).astype(jnp.bfloat16)
    out_pre = conv_layer(w_last, active_two).reshape(-1)
    out_tan = conv_layer(w_last, tan_two).reshape(-1)
    denoised = pushed_one - out_pre
    probe_vals = probe_one.astype(jnp.float32)
    spread = jnp.mean(probe_vals * (probe_vals - out_tan))
    return (denoised, spread)

def reference(transfer, observed, start, probe, w_first, w_mid, w_last):
    trace = jnp.sum(transfer * transfer)
    estimate = start
    for iteration in range(ITERS):
        fitted = jnp.dot(estimate, transfer.T, precision=lax.Precision.HIGHEST, preferred_element_type=jnp.float32)
        misfit = observed - fitted
        squares = lax.optimization_barrier(jnp.sum(misfit * misfit, axis=1))
        levels = jnp.sqrt(squares / trace)
        back_sum = jnp.dot(misfit, transfer, precision=lax.Precision.HIGHEST, preferred_element_type=jnp.float32)
        pushed = estimate + PIX / trace * back_sum
        denoised, spread = lax.map(lambda bundle: denoise(bundle, w_first, w_mid, w_last), (pushed, levels, probe))
        onsager = denoised - spread[:, None] * pushed
        gains = lax.optimization_barrier(jnp.sum(denoised * onsager, axis=1)) / (lax.optimization_barrier(jnp.sum(onsager * onsager, axis=1)) + 1e-06)
        estimate = gains[:, None] * onsager
    return estimate
```

```python
import jax
import jax.numpy as jnp
from jax import lax
from jax.sharding import Mesh
from jax.sharding import PartitionSpec as P

IMG = 128
ITERS = 2
PIX = 16384
ROW_AXES = ("xh", "y", "c")
MODE_AXES = ("xl", "z")
SWAP = [(0, 1), (1, 0)]
EXT = 128


def conv_layer(weights, feature):
    in_chan, extent_rows, extent_cols = feature.shape
    out_chan = weights.shape[1]
    padded = jnp.pad(feature, ((0, 0), (1, 1), (1, 1)))
    if out_chan == 1:
        taps_flat = weights[:, 0, :]
        products = jnp.dot(
            taps_flat,
            feature.reshape(in_chan, extent_rows * extent_cols),
            preferred_element_type=jnp.float32,
        )
        products = jnp.pad(products.reshape(9, extent_rows, extent_cols), ((0, 0), (1, 1), (1, 1)))
        summed = jnp.zeros((extent_rows, extent_cols), jnp.float32)
        for offset in range(9):
            row_shift = offset // 3
            col_shift = offset % 3
            summed = (
                summed
                + products[
                    offset, row_shift : row_shift + extent_rows, col_shift : col_shift + extent_cols
                ]
            )
        return summed.reshape(1, extent_rows, extent_cols)
    windows = []
    for offset in range(9):
        row_shift = offset // 3
        col_shift = offset % 3
        windows.append(
            padded[:, row_shift : row_shift + extent_rows, col_shift : col_shift + extent_cols]
        )
    columns = jnp.concatenate(windows, axis=0).reshape(9 * in_chan, extent_rows * extent_cols)
    weight_flat = jnp.transpose(weights, (1, 0, 2)).reshape(out_chan, 9 * in_chan)
    summed = jnp.dot(weight_flat, columns, preferred_element_type=jnp.float32)
    return summed.reshape(out_chan, extent_rows, extent_cols)


def silu_slope(values):
    logistic = jax.nn.sigmoid(values)
    return logistic * (1.0 + values * (1.0 - logistic))


def denoise(pushed_one, levels_one, probe_one, w_first, w_mid, w_last):
    picture = pushed_one.reshape(IMG, IMG)
    stacked = jnp.stack([picture, jnp.zeros_like(picture) + levels_one]).astype(jnp.bfloat16)
    first_pre = conv_layer(w_first, stacked)
    first_tan = conv_layer(w_first[:, :, 0:1], probe_one.reshape(1, IMG, IMG))
    active_one = jax.nn.silu(first_pre).astype(jnp.bfloat16)
    tan_one = (silu_slope(first_pre) * first_tan).astype(jnp.bfloat16)
    second_pre = conv_layer(w_mid, active_one)
    second_tan = conv_layer(w_mid, tan_one)
    active_two = jax.nn.silu(second_pre).astype(jnp.bfloat16)
    tan_two = (silu_slope(second_pre) * second_tan).astype(jnp.bfloat16)
    out_pre = conv_layer(w_last, active_two).reshape(-1)
    out_tan = conv_layer(w_last, tan_two).reshape(-1)
    denoised = pushed_one - out_pre
    probe_vals = probe_one.astype(jnp.float32)
    spread = jnp.mean(probe_vals * (probe_vals - out_tan))
    onsager = denoised - spread * pushed_one
    gain = jnp.sum(denoised * onsager) / (jnp.sum(onsager * onsager) + 1e-06)
    return gain * onsager


def gather_rows(block):
    copies = jnp.broadcast_to(block[None], (8,) + block.shape)
    own = lax.all_to_all(copies, ("xh", "y"), 0, 0, tiled=True)
    other = lax.ppermute(own, "c", SWAP)
    first = lax.axis_index("c") == 0
    both = jnp.stack([jnp.where(first, own, other), jnp.where(first, other, own)], axis=1)
    return both.reshape(-1, block.shape[1])


def sum_rows(parts):
    halves = parts.reshape(8, 2, 16, -1)
    first = lax.axis_index("c") == 0
    mine = jnp.where(first, halves[:, 0], halves[:, 1])
    theirs = jnp.where(first, halves[:, 1], halves[:, 0])
    mine = mine + lax.ppermute(theirs, "c", SWAP)
    return jnp.sum(lax.all_to_all(mine, ("xh", "y"), 0, 0, tiled=True), axis=0)


def sum_modes(parts):
    shares = lax.all_to_all(parts.reshape(16, 16, -1), MODE_AXES, 0, 0, tiled=True)
    return jnp.sum(shares, axis=0)


def gather_modes(block):
    copies = jnp.broadcast_to(block[None], (16,) + block.shape)
    return lax.all_to_all(copies, MODE_AXES, 0, 0, tiled=True).reshape(-1, block.shape[1])


def frames_whole(block):
    return lax.all_to_all(block, MODE_AXES, 0, 0, tiled=True)


def body(transfer, observed, start, probe, w_first, w_mid, w_last):
    mode_index = lax.axis_index("xl") * 8 + lax.axis_index("z")
    share = jnp.sum(transfer * transfer)
    estimate = start
    whole = None
    recovered = None
    trace = None
    for iteration in range(ITERS):
        if iteration == 0:
            extra = jnp.broadcast_to(share, (16, EXT))
            gathered = gather_rows(jnp.concatenate([estimate, extra], axis=1))
            all_estimates = gathered[:, :1024]
            share = jnp.sum(gathered[:, 1024].reshape(16, 16)[:, 0])
        else:
            all_estimates = gather_rows(estimate)
        partial_value = lax.dot_general(
            all_estimates,
            transfer,
            (((1,), (1,)), ((), ())),
            precision=lax.Precision.HIGHEST,
            preferred_element_type=jnp.float32,
        )
        misfit = observed - sum_modes(partial_value)
        misfit_all = gather_modes(misfit)
        square_part = jnp.sum(misfit_all * misfit_all, axis=1, keepdims=True)
        back_part = jnp.dot(
            misfit_all,
            transfer,
            precision=lax.Precision.HIGHEST,
            preferred_element_type=jnp.float32,
        )
        summed = sum_rows(
            jnp.concatenate([back_part, jnp.broadcast_to(square_part, (256, EXT))], axis=1)
        )
        back_sum = summed[:, :1024]
        squares = lax.dynamic_slice(summed[:, 1024], (mode_index,), (1,))[0]
        if iteration == 0:
            extra = jnp.broadcast_to(share, (16, EXT))
            mixed = frames_whole(jnp.concatenate([start, back_sum, extra], axis=1))
            whole = mixed[:, :1024].reshape(-1)
            back = mixed[:, 1024:2048].reshape(-1)
            trace = jnp.sum(mixed[:, 2048])
        else:
            back = frames_whole(back_sum).reshape(-1)
        pushed = whole + PIX / trace * back
        level = jnp.sqrt(squares / trace)
        recovered = denoise(pushed, level, probe[0], w_first, w_mid, w_last)
        whole = recovered
        if iteration + 1 < ITERS:
            estimate = lax.all_to_all(recovered.reshape(16, 1024), MODE_AXES, 0, 0, tiled=True)
    return recovered[None]


def solution(mesh):
    fine = Mesh(mesh.devices.reshape(2, 4, 2, 2, 8), ROW_AXES + MODE_AXES)
    return jax.shard_map(
        body,
        mesh=fine,
        in_specs=(
            P(ROW_AXES, MODE_AXES),
            P(MODE_AXES, ROW_AXES),
            P(ROW_AXES, MODE_AXES),
            P(ROW_AXES + MODE_AXES, None),
            P(),
            P(),
            P(),
        ),
        out_specs=P(ROW_AXES + MODE_AXES, None),
        check_vma=False,
    )
```

```python
import functools

import jax
import jax.numpy as jnp
from jax import lax
from jax.experimental import pallas as pl
from jax.experimental.pallas import tpu as pltpu
from jax.sharding import Mesh
from jax.sharding import PartitionSpec as P

IMG = 128
ITERS = 2
PIX = 16384
ROW_AXES = ("xh", "y", "c")
MODE_AXES = ("xl", "z")
SWAP = [(0, 1), (1, 0)]
EXT = 128
PLANE = ("xh", "y", "xl")
WIDE = 1024 + EXT


CH = 48
LANES = 128


def left_of(value, lane):
    return jnp.where(lane == 0, 0.0, pltpu.roll(value, 1, 1))


def right_of(value, lane):
    return jnp.where(lane == LANES - 1, 0.0, pltpu.roll(value, LANES - 1, 1))


def shifted(value, lane):
    return left_of(value, lane), value, right_of(value, lane)


def silu_and_tangent(value, tangent):
    logistic = 0.5 * jnp.tanh(0.5 * value) + 0.5
    active = value * logistic
    slope = logistic + active * (1.0 - logistic)
    return active, slope * tangent


def denoise_kernel(
    back_at,
    flat_out,
    whole_ref,
    back_ref,
    base_ref,
    probe_ref,
    first_ref,
    mid_ref,
    last_ref,
    out_ref,
    pushed_ref,
    pads_ref,
    prim_ref,
    tang_ref,
    taps_ref,
):
    lane = lax.broadcasted_iota(jnp.int32, (IMG, LANES), 1)
    lane_ch = lax.broadcasted_iota(jnp.int32, (CH, LANES), 1)
    ends = lax.broadcasted_iota(jnp.int32, (8, EXT), 1) == EXT - 1
    shares = base_ref[:, pl.ds(2048 + 1024, EXT)] + base_ref[:, pl.ds(2048 + WIDE + 1024, EXT)]
    trace = jnp.zeros((8, LANES), jnp.float32) + jnp.sum(jnp.where(ends, shares, 0.0))
    squares = jnp.zeros((IMG, LANES), jnp.float32) + back_ref[0:1, pl.ds(back_at + 1024, 1)]
    level = jnp.sqrt(squares / trace[0:1, :])
    scale = PIX / trace
    for side in range(2):
        for part in range(8):
            rows = (
                whole_ref[:, pl.ds(side * 1024 + part * LANES, LANES)]
                + scale * back_ref[:, pl.ds(back_at + side * WIDE + part * LANES, LANES)]
            )
            pushed_ref[pl.ds(side * 64 + part, 8, stride=8), :] = rows
    pushed = pushed_ref[...]
    border = jnp.zeros((8, LANES), jnp.float32)
    for group, picture in enumerate((pushed, level, probe_ref[...])):
        for step, moved in enumerate(shifted(picture, lane)):
            pads_ref[group * 3 + step, 0:8, :] = border
            pads_ref[group * 3 + step, 8:136, :] = moved
            pads_ref[group * 3 + step, 136:144, :] = border
    blank = jnp.zeros((3 * CH, LANES), jnp.bfloat16)
    for store in (prim_ref, tang_ref):
        store[0] = blank
        store[IMG + 1] = blank
    taps_ref[0:32, :] = jnp.zeros((32, LANES), jnp.float32)
    taps_ref[(IMG + 1) * 32 : (IMG + 2) * 32, :] = jnp.zeros((32, LANES), jnp.float32)

    def window(groups, base):
        return jnp.concatenate(
            [pads_ref[slot, pl.ds(base, 32), :].astype(jnp.bfloat16) for slot in groups], axis=0
        )

    @pl.loop(0, 4)
    def _(block):
        base = pl.multiple_of(block * 32, 32)
        seen = jnp.concatenate([window(range(6), base), window(range(6), base + 16)], axis=1)
        probed = jnp.concatenate([window(range(6, 9), base), window(range(6, 9), base + 16)], axis=1)
        values = jnp.dot(first_ref[...], seen, preferred_element_type=jnp.float32)
        tangents = jnp.dot(first_ref[:, 0:96], probed, preferred_element_type=jnp.float32)
        for half in range(2):
            cols = slice(half * LANES, (half + 1) * LANES)
            for row in range(16):
                rows = slice(row * CH, (row + 1) * CH)
                active, tangent = silu_and_tangent(values[rows, cols], tangents[rows, cols])
                at = base + half * 16 + row + 1
                for store, value in ((prim_ref, active), (tang_ref, tangent)):
                    for step, moved in enumerate(shifted(value, lane_ch)):
                        store[at, step * CH : (step + 1) * CH, :] = moved.astype(jnp.bfloat16)

    def products(store, start, count):
        rows = jnp.concatenate([store[start + k] for k in range(count)], axis=1)
        return jnp.dot(mid_ref[...], rows, preferred_element_type=jnp.float32)

    def piece(prod, tap, k):
        return prod[tap * CH : (tap + 1) * CH, k * LANES : (k + 1) * LANES]

    def primed(store):
        prod = products(store, 0, 2)
        return piece(prod, 0, 0) + piece(prod, 1, 1), piece(prod, 0, 1)

    def step(index, carry):
        start = index * 8 + 2
        made = []
        fresh = []
        for store, (older, old) in zip((prim_ref, tang_ref), carry):
            prod = products(store, start, 8)
            rows = []
            for k in range(8):
                rows.append(older + piece(prod, 2, k))
                older = old + piece(prod, 1, k)
                old = piece(prod, 0, k)
            made.append(rows)
            fresh.append((older, old))
        stacked = []
        for value, tangent in zip(*made):
            active, tangent = silu_and_tangent(value, tangent)
            stacked.append(
                jnp.concatenate([active.astype(jnp.bfloat16), tangent.astype(jnp.bfloat16)], axis=0)
            )
        taps = jnp.dot(
            last_ref[...], jnp.concatenate(stacked, axis=1), preferred_element_type=jnp.float32
        )
        for k in range(8):
            at = pl.multiple_of((start - 1 + k) * 32, 32)
            taps_ref[pl.ds(at, 32), :] = taps[:, k * LANES : (k + 1) * LANES]
        return tuple(fresh)

    lax.fori_loop(0, 16, step, (primed(prim_ref), primed(tang_ref)))

    def gathered(first_tap):
        sums = []
        for col in range(3):
            total = None
            for row in range(3):
                tap = first_tap + row * 3 + col
                term = taps_ref[pl.ds(row * 32 + tap, IMG, stride=32), :]
                total = term if total is None else total + term
            sums.append(total)
        return left_of(sums[0], lane) + sums[1] + right_of(sums[2], lane)

    denoised = pushed_ref[...] - gathered(0)
    probe = probe_ref[...]
    spread = jnp.sum(probe * (probe - gathered(9))) / PIX
    onsager = denoised - spread * pushed_ref[...]
    gain = jnp.sum(denoised * onsager) / (jnp.sum(onsager * onsager) + 1e-06)
    recovered = gain * onsager
    pushed_ref[...] = recovered
    if flat_out:
        for row in range(IMG):
            out_ref[0:1, row * LANES : (row + 1) * LANES] = pushed_ref[row : row + 1, :]
    else:
        for part in range(16):
            start = part // 8 * 64 + part % 8
            out_ref[:, part * LANES : (part + 1) * LANES] = pushed_ref[pl.ds(start, 8, stride=8), :]


def weights_ready(w_first, w_mid, w_last):
    tap = jnp.arange(3)[:, None, None]
    row = jnp.arange(16)[None, :, None]
    source = jnp.arange(32)[None, None, :]
    places = (source == row + 7 + tap).astype(jnp.bfloat16)
    first = jnp.einsum(
        "khj,kdoi->hoidj", places, w_first.reshape(3, 3, CH, 2), preferred_element_type=jnp.float32
    )
    first = first.astype(jnp.bfloat16).reshape(16 * CH, 192)
    mid = jnp.transpose(w_mid.reshape(3, 3, CH, CH), (0, 2, 1, 3)).reshape(3 * CH, 3 * CH)
    taps = w_last[:, 0, :]
    blank = jnp.zeros((9, CH), jnp.bfloat16)
    last = jnp.concatenate(
        [
            jnp.concatenate([taps, blank], axis=1),
            jnp.concatenate([blank, taps], axis=1),
            jnp.zeros((14, 2 * CH), jnp.bfloat16),
        ],
        axis=0,
    )
    return first, mid, last


def denoise(whole, back, back_at, base, probe, weights, flat_out):
    vmem = pl.BlockSpec(memory_space=pltpu.VMEM)
    return pl.pallas_call(
        functools.partial(denoise_kernel, back_at, flat_out),
        out_shape=jax.ShapeDtypeStruct((1, PIX) if flat_out else (8, 2048), jnp.float32),
        in_specs=[vmem] * 7,
        out_specs=vmem,
        scratch_shapes=[
            pltpu.VMEM((IMG, LANES), jnp.float32),
            pltpu.VMEM((9, IMG + 16, LANES), jnp.float32),
            pltpu.VMEM((IMG + 2, 3 * CH, LANES), jnp.bfloat16),
            pltpu.VMEM((IMG + 2, 3 * CH, LANES), jnp.bfloat16),
            pltpu.VMEM(((IMG + 2) * 32, LANES), jnp.float32),
        ],
        compiler_params=pltpu.CompilerParams(vmem_limit_bytes=32 << 20),
        name="denoise",
    )(whole, back, base, probe, *weights)


def times(block, transfer, axis):
    return lax.dot_general(
        block,
        transfer,
        (((1,), (axis,)), ((), ())),
        precision=lax.Precision.HIGH,
        preferred_element_type=jnp.float32,
    )


def times(block, transfer, axis):
    return lax.dot_general(
        block,
        transfer,
        (((1,), (axis,)), ((), ())),
        precision=lax.Precision.HIGHEST,
        preferred_element_type=jnp.float32,
    )


def with_core(own):
    other = lax.ppermute(own, "c", SWAP)
    first = lax.axis_index("c") == 0
    both = jnp.stack([jnp.where(first, own, other), jnp.where(first, other, own)], axis=1)
    return both.reshape(16, 16, -1)


def gather_start(block):
    copies = jnp.broadcast_to(block[None], (8,) + block.shape)
    return with_core(lax.all_to_all(copies, ("xh", "y"), 0, 0, tiled=True))


def gather_whole(whole):
    rows = lax.all_to_all(whole, "z", 0, 0, tiled=True).reshape(8, -1)
    pair = jnp.stack([rows[:, :1024], rows[:, 1024:]])
    copies = jnp.broadcast_to(pair[None], (8, 2, 8, 1024)).reshape(16, 8, 1024)
    return with_core(lax.all_to_all(copies, PLANE, 0, 0, tiled=True).reshape(8, 16, 1024))


def fitted_share(blocks, transfer):
    made = times(blocks.reshape(256, -1), transfer, 1)
    shares = lax.all_to_all(made.reshape(16, 16, -1), MODE_AXES, 0, 0, tiled=True)
    return jnp.sum(shares, axis=0)


def adjoint_share(misfit, transfer, share):
    copies = jnp.broadcast_to(misfit[None], (8,) + misfit.shape)
    own = lax.all_to_all(copies, "z", 0, 0, tiled=True).reshape(128, -1)
    other = lax.ppermute(own, "xl", SWAP)
    first_core = lax.axis_index("c") == 0
    lane = lax.broadcasted_iota(jnp.int32, (128, EXT), 1)
    halves = []
    for rows in (own, other):
        squares = jnp.sum(rows * rows, axis=1, keepdims=True)
        made = jnp.concatenate(
            [times(rows, transfer, 0), jnp.where(lane < EXT // 2, squares, share)], axis=1
        ).reshape(4, 2, 16, -1)
        mine = jnp.where(first_core, made[:, 0], made[:, 1])
        theirs = jnp.where(first_core, made[:, 1], made[:, 0])
        halves.append(mine + lax.ppermute(theirs, "c", SWAP))
    first = lax.axis_index("xl") == 0
    ordered = jnp.where(first, jnp.concatenate(halves), jnp.concatenate(halves[::-1]))
    parts = lax.all_to_all(ordered.reshape(16, 8, -1), PLANE, 0, 0, tiled=True)
    summed = jnp.sum(parts.reshape(8, 2, 8, -1), axis=0)
    return jnp.concatenate([summed[0], summed[1]], axis=1)


def exchange_z(block):
    return lax.all_to_all(block, "z", 0, 0, tiled=True)


def body(transfer, observed, start, probe, w_first, w_mid, w_last):
    weights = weights_ready(w_first, w_mid, w_last)
    picture = probe.reshape(IMG, IMG).astype(jnp.float32)
    first = lax.axis_index("xl") == 0
    kept = jnp.where(first, start[:8], start[8:])
    moved = lax.ppermute(jnp.where(first, start[8:], start[:8]), "xl", SWAP)
    start_pair = jnp.concatenate(
        [jnp.where(first, kept, moved), jnp.where(first, moved, kept)], axis=1
    )
    share = jnp.sum(transfer * transfer)
    blocks = gather_start(start)
    whole = None
    base = None
    for iteration in range(ITERS):
        misfit = observed - fitted_share(blocks, transfer)
        summed = adjoint_share(misfit, transfer, share)
        last = iteration + 1 == ITERS
        if iteration == 0:
            base = exchange_z(jnp.concatenate([start_pair, summed], axis=1))
            whole = denoise(base, base, 2048, base, picture, weights, last)
        else:
            whole = denoise(whole, exchange_z(summed), 0, base, picture, weights, last)
        if not last:
            blocks = gather_whole(whole)
    return whole


def solution(mesh):
    fine = Mesh(mesh.devices.reshape(2, 4, 2, 2, 8), ROW_AXES + MODE_AXES)
    return jax.shard_map(
        body,
        mesh=fine,
        in_specs=(
            P(ROW_AXES, MODE_AXES),
            P(MODE_AXES, ROW_AXES),
            P(ROW_AXES, MODE_AXES),
            P(ROW_AXES + MODE_AXES, None),
            P(),
            P(),
            P(),
        ),
        out_specs=P(ROW_AXES + MODE_AXES, None),
        check_vma=False,
    )
```

```python
import functools

import jax
import jax.numpy as jnp
from jax import lax
from jax.experimental import pallas as pl
from jax.experimental.pallas import tpu as pltpu
from jax.sharding import Mesh
from jax.sharding import PartitionSpec as P

IMG = 128
ITERS = 2
PIX = 16384
ROW_AXES = ("xh", "y", "c")
MODE_AXES = ("xl", "z")
SWAP = [(0, 1), (1, 0)]
EXT = 128
PLANE = ("xh", "y", "xl")
WIDE = 1024 + EXT


CH = 48
LANES = 128
TALL = 136
GROUP = 32


def left_of(value, lane):
    return jnp.where(lane == 0, 0.0, pltpu.roll(value, 1, 1))


def right_of(value, lane):
    return jnp.where(lane == LANES - 1, 0.0, pltpu.roll(value, LANES - 1, 1))


def shifted(value, lane):
    return left_of(value, lane), value, right_of(value, lane)


def silu_and_tangent(value, tangent):
    logistic = 0.5 * jnp.tanh(0.5 * value) + 0.5
    active = value * logistic
    slope = logistic + active * (1.0 - logistic)
    return active, slope * tangent


def denoise_kernel(
    back_at,
    flat_out,
    whole_ref,
    back_ref,
    base_ref,
    probe_ref,
    first_ref,
    mid_ref,
    last_ref,
    out_ref,
    pushed_ref,
    pads_ref,
    prim_ref,
    tang_ref,
    taps_ref,
):
    lane = lax.broadcasted_iota(jnp.int32, (IMG, LANES), 1)
    lane_ch = lax.broadcasted_iota(jnp.int32, (CH, LANES), 1)
    ends = lax.broadcasted_iota(jnp.int32, (8, EXT), 1) == EXT - 1
    shares = base_ref[:, pl.ds(2048 + 1024, EXT)] + base_ref[:, pl.ds(2048 + WIDE + 1024, EXT)]
    trace = jnp.zeros((8, LANES), jnp.float32) + jnp.sum(jnp.where(ends, shares, 0.0))
    squares = jnp.zeros((IMG, LANES), jnp.float32) + back_ref[0:1, pl.ds(back_at + 1024, 1)]
    level = jnp.sqrt(squares / trace[0:1, :])
    scale = PIX / trace
    for side in range(2):
        for part in range(8):
            rows = (
                whole_ref[:, pl.ds(side * 1024 + part * LANES, LANES)]
                + scale * back_ref[:, pl.ds(back_at + side * WIDE + part * LANES, LANES)]
            )
            pushed_ref[pl.ds(side * 64 + part, 8, stride=8), :] = rows
    pushed = pushed_ref[...]
    border = jnp.zeros((8, LANES), jnp.float32)
    for group, picture in enumerate((pushed, level, probe_ref[...])):
        for step, moved in enumerate(shifted(picture, lane)):
            pads_ref[group * 3 + step, 0:8, :] = border
            pads_ref[group * 3 + step, 8:136, :] = moved
            pads_ref[group * 3 + step, 136:144, :] = border
    blank = jnp.zeros((3 * CH, LANES), jnp.bfloat16)
    for store in (prim_ref, tang_ref):
        store[0] = blank
        store[IMG + 1] = blank
    for tap in range(18):
        taps_ref[tap * TALL : tap * TALL + 1, :] = jnp.zeros((1, LANES), jnp.float32)
        taps_ref[tap * TALL + IMG + 1 : tap * TALL + IMG + 2, :] = jnp.zeros((1, LANES), jnp.float32)

    def window(groups, base):
        return jnp.concatenate(
            [pads_ref[slot, pl.ds(base, 32), :].astype(jnp.bfloat16) for slot in groups], axis=0
        )

    @pl.loop(0, 4)
    def _(block):
        base = pl.multiple_of(block * 32, 32)
        seen = jnp.concatenate([window(range(6), base), window(range(6), base + 16)], axis=1)
        probed = jnp.concatenate([window(range(6, 9), base), window(range(6, 9), base + 16)], axis=1)
        values = jnp.dot(first_ref[...], seen, preferred_element_type=jnp.float32)
        tangents = jnp.dot(first_ref[:, 0:96], probed, preferred_element_type=jnp.float32)
        for half in range(2):
            cols = slice(half * LANES, (half + 1) * LANES)
            for row in range(16):
                rows = slice(row * CH, (row + 1) * CH)
                active, tangent = silu_and_tangent(values[rows, cols], tangents[rows, cols])
                at = base + half * 16 + row + 1
                for store, value in ((prim_ref, active), (tang_ref, tangent)):
                    for step, moved in enumerate(shifted(value, lane_ch)):
                        store[at, step * CH : (step + 1) * CH, :] = moved.astype(jnp.bfloat16)

    def products(store, start, count):
        rows = jnp.concatenate([store[start + k] for k in range(count)], axis=1)
        return jnp.dot(mid_ref[...], rows, preferred_element_type=jnp.float32)

    def piece(prod, tap, k):
        return prod[tap * CH : (tap + 1) * CH, k * LANES : (k + 1) * LANES]

    def primed(store):
        prod = products(store, 0, 2)
        return piece(prod, 0, 0) + piece(prod, 1, 1), piece(prod, 0, 1)

    def step(index, carry):
        start = index * GROUP + 2
        made = []
        fresh = []
        for store, (older, old) in zip((prim_ref, tang_ref), carry):
            prod = products(store, start, GROUP)
            rows = []
            for k in range(GROUP):
                rows.append(older + piece(prod, 2, k))
                older = old + piece(prod, 1, k)
                old = piece(prod, 0, k)
            made.append(rows)
            fresh.append((older, old))
        stacked = []
        for value, tangent in zip(*made):
            active, tangent = silu_and_tangent(value, tangent)
            stacked.append(
                jnp.concatenate([active.astype(jnp.bfloat16), tangent.astype(jnp.bfloat16)], axis=0)
            )
        taps = jnp.dot(
            last_ref[...], jnp.concatenate(stacked, axis=1), preferred_element_type=jnp.float32
        )
        for k in range(GROUP):
            taps_ref[pl.ds(start - 1 + k, 24, stride=TALL), :] = taps[
                :24, k * LANES : (k + 1) * LANES
            ]
        return tuple(fresh)

    lax.fori_loop(0, IMG // GROUP, step, (primed(prim_ref), primed(tang_ref)))

    def gathered(first_tap):
        sums = []
        for col in range(3):
            total = None
            for row in range(3):
                tap = first_tap + row * 3 + col
                term = taps_ref[pl.ds(tap * TALL + row, IMG), :]
                total = term if total is None else total + term
            sums.append(total)
        return left_of(sums[0], lane) + sums[1] + right_of(sums[2], lane)

    denoised = pushed_ref[...] - gathered(0)
    probe = probe_ref[...]
    spread = jnp.sum(probe * (probe - gathered(9))) / PIX
    onsager = denoised - spread * pushed_ref[...]
    gain = jnp.sum(denoised * onsager) / (jnp.sum(onsager * onsager) + 1e-06)
    recovered = gain * onsager
    pushed_ref[...] = recovered
    if flat_out:
        for row in range(IMG):
            out_ref[0:1, row * LANES : (row + 1) * LANES] = pushed_ref[row : row + 1, :]
    else:
        for part in range(16):
            start = part // 8 * 64 + part % 8
            out_ref[:, part * LANES : (part + 1) * LANES] = pushed_ref[pl.ds(start, 8, stride=8), :]


def weights_ready(w_first, w_mid, w_last):
    tap = jnp.arange(3)[:, None, None]
    row = jnp.arange(16)[None, :, None]
    source = jnp.arange(32)[None, None, :]
    places = (source == row + 7 + tap).astype(jnp.bfloat16)
    first = jnp.einsum(
        "khj,kdoi->hoidj", places, w_first.reshape(3, 3, CH, 2), preferred_element_type=jnp.float32
    )
    first = first.astype(jnp.bfloat16).reshape(16 * CH, 192)
    mid = jnp.transpose(w_mid.reshape(3, 3, CH, CH), (0, 2, 1, 3)).reshape(3 * CH, 3 * CH)
    taps = w_last[:, 0, :]
    blank = jnp.zeros((9, CH), jnp.bfloat16)
    last = jnp.concatenate(
        [
            jnp.concatenate([taps, blank], axis=1),
            jnp.concatenate([blank, taps], axis=1),
            jnp.zeros((14, 2 * CH), jnp.bfloat16),
        ],
        axis=0,
    )
    return first, mid, last


def denoise(whole, back, back_at, base, probe, weights, flat_out):
    vmem = pl.BlockSpec(memory_space=pltpu.VMEM)
    return pl.pallas_call(
        functools.partial(denoise_kernel, back_at, flat_out),
        out_shape=jax.ShapeDtypeStruct((1, PIX) if flat_out else (8, 2048), jnp.float32),
        in_specs=[vmem] * 7,
        out_specs=vmem,
        scratch_shapes=[
            pltpu.VMEM((IMG, LANES), jnp.float32),
            pltpu.VMEM((9, IMG + 16, LANES), jnp.float32),
            pltpu.VMEM((IMG + 2, 3 * CH, LANES), jnp.bfloat16),
            pltpu.VMEM((IMG + 2, 3 * CH, LANES), jnp.bfloat16),
            pltpu.VMEM((24 * TALL, LANES), jnp.float32),
        ],
        compiler_params=pltpu.CompilerParams(vmem_limit_bytes=32 << 20),
        name="denoise",
    )(whole, back, base, probe, *weights)


def times(block, transfer, axis):
    return lax.dot_general(
        block,
        transfer,
        (((1,), (axis,)), ((), ())),
        precision=lax.Precision.HIGH,
        preferred_element_type=jnp.float32,
    )


def times(block, transfer, axis):
    return lax.dot_general(
        block,
        transfer,
        (((1,), (axis,)), ((), ())),
        precision=lax.Precision.HIGHEST,
        preferred_element_type=jnp.float32,
    )


def with_core(own):
    other = lax.ppermute(own, "c", SWAP)
    first = lax.axis_index("c") == 0
    both = jnp.stack([jnp.where(first, own, other), jnp.where(first, other, own)], axis=1)
    return both.reshape(16, 16, -1)


def gather_start(block):
    copies = jnp.broadcast_to(block[None], (8,) + block.shape)
    return with_core(lax.all_to_all(copies, ("xh", "y"), 0, 0, tiled=True))


def gather_whole(whole):
    rows = lax.all_to_all(whole, "z", 0, 0, tiled=True).reshape(8, -1)
    pair = jnp.stack([rows[:, :1024], rows[:, 1024:]])
    copies = jnp.broadcast_to(pair[None], (8, 2, 8, 1024)).reshape(16, 8, 1024)
    return with_core(lax.all_to_all(copies, PLANE, 0, 0, tiled=True).reshape(8, 16, 1024))


def along_z(value, ahead):
    return lax.ppermute(value, "z", [(i, (i + ahead) % 8) for i in range(8)])


def across(value):
    return lax.ppermute(value, "xl", SWAP)


def fitted_share(blocks, transfer):
    z, xl = lax.axis_index("z"), lax.axis_index("xl")
    made = times(blocks.reshape(256, -1), transfer, 1).reshape(2, 8, 16, -1)

    def pick(side, ahead):
        at = (xl if side == 0 else 1 - xl, (z + ahead + 8) % 8, 0, 0)
        return lax.dynamic_slice(made, at, (1, 1, 16, made.shape[3]))[0, 0]

    distant = across(jnp.concatenate([pick(1, ahead) for ahead in (3, -3, 4)]))
    close = across(jnp.concatenate([pick(1, ahead) for ahead in (2, -2, 1, -1, 0)]))
    up3 = along_z(pick(0, 3) + distant[:16], 1)
    down3 = along_z(pick(0, -3) + distant[16:32], -1)
    up4 = along_z(pick(0, 4) + distant[32:], 2)
    up1 = along_z(pick(0, 1) + close[32:48], 1)
    down1 = along_z(pick(0, -1) + close[48:64], -1)
    up2 = along_z(pick(0, 2) + close[:16] + up3 + up4, 2)
    down2 = along_z(pick(0, -2) + close[16:32] + down3, -2)
    return pick(0, 0) + close[64:] + up1 + down1 + up2 + down2


def adjoint_share(misfit, transfer, share):
    copies = jnp.broadcast_to(misfit[None], (8,) + misfit.shape)
    own = lax.all_to_all(copies, "z", 0, 0, tiled=True).reshape(128, -1)
    other = lax.ppermute(own, "xl", SWAP)
    first_core = lax.axis_index("c") == 0
    lane = lax.broadcasted_iota(jnp.int32, (128, EXT), 1)
    halves = []
    for rows in (own, other):
        squares = jnp.sum(rows * rows, axis=1, keepdims=True)
        made = jnp.concatenate(
            [times(rows, transfer, 0), jnp.where(lane < EXT // 2, squares, share)], axis=1
        ).reshape(4, 2, 16, -1)
        mine = jnp.where(first_core, made[:, 0], made[:, 1])
        theirs = jnp.where(first_core, made[:, 1], made[:, 0])
        halves.append(mine + lax.ppermute(theirs, "c", SWAP))
    first = lax.axis_index("xl") == 0
    ordered = jnp.where(first, jnp.concatenate(halves), jnp.concatenate(halves[::-1]))
    parts = lax.all_to_all(ordered.reshape(16, 8, -1), PLANE, 0, 0, tiled=True)
    summed = jnp.sum(parts.reshape(8, 2, 8, -1), axis=0)
    return jnp.concatenate([summed[0], summed[1]], axis=1)


def exchange_z(block):
    return lax.all_to_all(block, "z", 0, 0, tiled=True)


def body(transfer, observed, start, probe, w_first, w_mid, w_last):
    weights = weights_ready(w_first, w_mid, w_last)
    picture = probe.reshape(IMG, IMG).astype(jnp.float32)
    first = lax.axis_index("xl") == 0
    kept = jnp.where(first, start[:8], start[8:])
    moved = lax.ppermute(jnp.where(first, start[8:], start[:8]), "xl", SWAP)
    start_pair = jnp.concatenate(
        [jnp.where(first, kept, moved), jnp.where(first, moved, kept)], axis=1
    )
    share = jnp.sum(transfer * transfer)
    blocks = gather_start(start)
    whole = None
    base = None
    for iteration in range(ITERS):
        misfit = observed - fitted_share(blocks, transfer)
        summed = adjoint_share(misfit, transfer, share)
        last = iteration + 1 == ITERS
        if iteration == 0:
            base = exchange_z(jnp.concatenate([start_pair, summed], axis=1))
            whole = denoise(base, base, 2048, base, picture, weights, last)
        else:
            whole = denoise(whole, exchange_z(summed), 0, base, picture, weights, last)
        if not last:
            blocks = gather_whole(whole)
    return whole


def solution(mesh):
    fine = Mesh(mesh.devices.reshape(2, 4, 2, 2, 8), ROW_AXES + MODE_AXES)
    return jax.shard_map(
        body,
        mesh=fine,
        in_specs=(
            P(ROW_AXES, MODE_AXES),
            P(MODE_AXES, ROW_AXES),
            P(ROW_AXES, MODE_AXES),
            P(ROW_AXES + MODE_AXES, None),
            P(),
            P(),
            P(),
        ),
        out_specs=P(ROW_AXES + MODE_AXES, None),
        check_vma=False,
    )
```

```python
import functools

import jax
import jax.numpy as jnp
from jax import lax
from jax.experimental import pallas as pl
from jax.experimental.pallas import tpu as pltpu
from jax.sharding import Mesh
from jax.sharding import PartitionSpec as P

IMG = 128
ITERS = 2
PIX = 16384
ROW_AXES = ("xh", "y", "c")
MODE_AXES = ("xl", "z")
SWAP = [(0, 1), (1, 0)]
EXT = 128
PLANE = ("xh", "y", "xl")
WIDE = 1024 + EXT


CH = 48
LANES = 128
TALL = 136
GROUP = 32


def left_of(value, lane):
    return jnp.where(lane == 0, 0.0, pltpu.roll(value, 1, 1))


def right_of(value, lane):
    return jnp.where(lane == LANES - 1, 0.0, pltpu.roll(value, LANES - 1, 1))


def shifted(value, lane):
    return left_of(value, lane), value, right_of(value, lane)


def silu_and_tangent(value, tangent):
    logistic = 0.5 * jnp.tanh(0.5 * value) + 0.5
    active = value * logistic
    slope = logistic + active * (1.0 - logistic)
    return active, slope * tangent


def denoise_kernel(
    back_at,
    flat_out,
    whole_ref,
    back_ref,
    base_ref,
    probe_ref,
    first_ref,
    mid_ref,
    last_ref,
    out_ref,
    pushed_ref,
    pads_ref,
    prim_ref,
    tang_ref,
    taps_ref,
):
    lane = lax.broadcasted_iota(jnp.int32, (IMG, LANES), 1)
    lane_ch = lax.broadcasted_iota(jnp.int32, (CH, LANES), 1)
    ends = lax.broadcasted_iota(jnp.int32, (8, EXT), 1) == EXT - 1
    shares = base_ref[:, pl.ds(2048 + 1024, EXT)] + base_ref[:, pl.ds(2048 + WIDE + 1024, EXT)]
    trace = jnp.zeros((8, LANES), jnp.float32) + jnp.sum(jnp.where(ends, shares, 0.0))
    squares = jnp.zeros((IMG, LANES), jnp.float32) + back_ref[0:1, pl.ds(back_at + 1024, 1)]
    level = jnp.sqrt(squares / trace[0:1, :])
    scale = PIX / trace
    for side in range(2):
        for part in range(8):
            rows = (
                whole_ref[:, pl.ds(side * 1024 + part * LANES, LANES)]
                + scale * back_ref[:, pl.ds(back_at + side * WIDE + part * LANES, LANES)]
            )
            pushed_ref[pl.ds(side * 64 + part, 8, stride=8), :] = rows
    pushed = pushed_ref[...]
    border = jnp.zeros((8, LANES), jnp.float32)
    for group, picture in enumerate((pushed, level, probe_ref[...])):
        for step, moved in enumerate(shifted(picture, lane)):
            pads_ref[group * 3 + step, 0:8, :] = border
            pads_ref[group * 3 + step, 8:136, :] = moved
            pads_ref[group * 3 + step, 136:144, :] = border
    blank = jnp.zeros((3 * CH, LANES), jnp.bfloat16)
    for store in (prim_ref, tang_ref):
        store[0] = blank
        store[IMG + 1] = blank
    for tap in range(18):
        taps_ref[tap * TALL : tap * TALL + 1, :] = jnp.zeros((1, LANES), jnp.float32)
        taps_ref[tap * TALL + IMG + 1 : tap * TALL + IMG + 2, :] = jnp.zeros((1, LANES), jnp.float32)

    def window(groups, base):
        return jnp.concatenate(
            [pads_ref[slot, pl.ds(base, 32), :].astype(jnp.bfloat16) for slot in groups], axis=0
        )

    @pl.loop(0, 4)
    def _(block):
        base = pl.multiple_of(block * 32, 32)
        seen = jnp.concatenate([window(range(6), base), window(range(6), base + 16)], axis=1)
        probed = jnp.concatenate([window(range(6, 9), base), window(range(6, 9), base + 16)], axis=1)
        values = jnp.dot(first_ref[...], seen, preferred_element_type=jnp.float32)
        tangents = jnp.dot(first_ref[:, 0:96], probed, preferred_element_type=jnp.float32)
        for half in range(2):
            cols = slice(half * LANES, (half + 1) * LANES)
            for row in range(16):
                rows = slice(row * CH, (row + 1) * CH)
                active, tangent = silu_and_tangent(values[rows, cols], tangents[rows, cols])
                at = base + half * 16 + row + 1
                for store, value in ((prim_ref, active), (tang_ref, tangent)):
                    for step, moved in enumerate(shifted(value, lane_ch)):
                        store[at, step * CH : (step + 1) * CH, :] = moved.astype(jnp.bfloat16)

    def products(store, start, count):
        rows = jnp.concatenate([store[start + k] for k in range(count)], axis=1)
        return jnp.dot(mid_ref[...], rows, preferred_element_type=jnp.float32)

    def piece(prod, tap, k):
        return prod[tap * CH : (tap + 1) * CH, k * LANES : (k + 1) * LANES]

    def primed(store):
        prod = products(store, 0, 2)
        return piece(prod, 0, 0) + piece(prod, 1, 1), piece(prod, 0, 1)

    def step(index, carry):
        start = index * GROUP + 2
        made = []
        fresh = []
        for store, (older, old) in zip((prim_ref, tang_ref), carry):
            prod = products(store, start, GROUP)
            rows = []
            for k in range(GROUP):
                rows.append(older + piece(prod, 2, k))
                older = old + piece(prod, 1, k)
                old = piece(prod, 0, k)
            made.append(rows)
            fresh.append((older, old))
        stacked = []
        for value, tangent in zip(*made):
            active, tangent = silu_and_tangent(value, tangent)
            stacked.append(
                jnp.concatenate([active.astype(jnp.bfloat16), tangent.astype(jnp.bfloat16)], axis=0)
            )
        taps = jnp.dot(
            last_ref[...], jnp.concatenate(stacked, axis=1), preferred_element_type=jnp.float32
        )
        for k in range(GROUP):
            taps_ref[pl.ds(start - 1 + k, 24, stride=TALL), :] = taps[
                :24, k * LANES : (k + 1) * LANES
            ]
        return tuple(fresh)

    lax.fori_loop(0, IMG // GROUP, step, (primed(prim_ref), primed(tang_ref)))

    def gathered(first_tap):
        sums = []
        for col in range(3):
            total = None
            for row in range(3):
                tap = first_tap + row * 3 + col
                term = taps_ref[pl.ds(tap * TALL + row, IMG), :]
                total = term if total is None else total + term
            sums.append(total)
        return left_of(sums[0], lane) + sums[1] + right_of(sums[2], lane)

    denoised = pushed_ref[...] - gathered(0)
    probe = probe_ref[...]
    spread = jnp.sum(probe * (probe - gathered(9))) / PIX
    onsager = denoised - spread * pushed_ref[...]
    gain = jnp.sum(denoised * onsager) / (jnp.sum(onsager * onsager) + 1e-06)
    recovered = gain * onsager
    pushed_ref[...] = recovered
    if flat_out:
        for row in range(IMG):
            out_ref[0:1, row * LANES : (row + 1) * LANES] = pushed_ref[row : row + 1, :]
    else:
        for part in range(16):
            start = part // 8 * 64 + part % 8
            out_ref[:, part * LANES : (part + 1) * LANES] = pushed_ref[pl.ds(start, 8, stride=8), :]


def weights_ready(w_first, w_mid, w_last):
    tap = jnp.arange(3)[:, None, None]
    row = jnp.arange(16)[None, :, None]
    source = jnp.arange(32)[None, None, :]
    places = (source == row + 7 + tap).astype(jnp.bfloat16)
    first = jnp.einsum(
        "khj,kdoi->hoidj", places, w_first.reshape(3, 3, CH, 2), preferred_element_type=jnp.float32
    )
    first = first.astype(jnp.bfloat16).reshape(16 * CH, 192)
    mid = jnp.transpose(w_mid.reshape(3, 3, CH, CH), (0, 2, 1, 3)).reshape(3 * CH, 3 * CH)
    taps = w_last[:, 0, :]
    blank = jnp.zeros((9, CH), jnp.bfloat16)
    last = jnp.concatenate(
        [
            jnp.concatenate([taps, blank], axis=1),
            jnp.concatenate([blank, taps], axis=1),
            jnp.zeros((14, 2 * CH), jnp.bfloat16),
        ],
        axis=0,
    )
    return first, mid, last


def denoise(whole, back, back_at, base, probe, weights, flat_out):
    vmem = pl.BlockSpec(memory_space=pltpu.VMEM)
    return pl.pallas_call(
        functools.partial(denoise_kernel, back_at, flat_out),
        out_shape=jax.ShapeDtypeStruct((1, PIX) if flat_out else (8, 2048), jnp.float32),
        in_specs=[vmem] * 7,
        out_specs=vmem,
        scratch_shapes=[
            pltpu.VMEM((IMG, LANES), jnp.float32),
            pltpu.VMEM((9, IMG + 16, LANES), jnp.float32),
            pltpu.VMEM((IMG + 2, 3 * CH, LANES), jnp.bfloat16),
            pltpu.VMEM((IMG + 2, 3 * CH, LANES), jnp.bfloat16),
            pltpu.VMEM((24 * TALL, LANES), jnp.float32),
        ],
        compiler_params=pltpu.CompilerParams(vmem_limit_bytes=32 << 20),
        name="denoise",
    )(whole, back, base, probe, *weights)


def times(block, transfer, axis):
    return lax.dot_general(
        block,
        transfer,
        (((1,), (axis,)), ((), ())),
        precision=lax.Precision.HIGH,
        preferred_element_type=jnp.float32,
    )


def times(block, transfer, axis):
    return lax.dot_general(
        block,
        transfer,
        (((1,), (axis,)), ((), ())),
        precision=lax.Precision.HIGHEST,
        preferred_element_type=jnp.float32,
    )


def with_core(own):
    other = lax.ppermute(own, "c", SWAP)
    first = lax.axis_index("c") == 0
    both = jnp.stack([jnp.where(first, own, other), jnp.where(first, other, own)], axis=1)
    return both.reshape(16, 16, -1)


def gather_start(block):
    copies = jnp.broadcast_to(block[None], (8,) + block.shape)
    return with_core(lax.all_to_all(copies, ("xh", "y"), 0, 0, tiled=True))


def gather_whole(whole):
    rows = lax.all_to_all(whole, "z", 0, 0, tiled=True).reshape(8, -1)
    pair = jnp.stack([rows[:, :1024], rows[:, 1024:]])
    copies = jnp.broadcast_to(pair[None], (8, 2, 8, 1024)).reshape(16, 8, 1024)
    return with_core(lax.all_to_all(copies, PLANE, 0, 0, tiled=True).reshape(8, 16, 1024))


def along_z(value, ahead):
    return lax.ppermute(value, "z", [(i, (i + ahead) % 8) for i in range(8)])


def across(value):
    return lax.ppermute(value, "xl", SWAP)


def fit_kernel(rows_ref, tile_ref, out_ref):
    out_ref[...] = times(rows_ref[...], tile_ref[...], 1)


def fit_products(rows, transfer):
    count, depth = rows.shape
    height = transfer.shape[0]
    return pl.pallas_call(
        fit_kernel,
        grid=(height // 256,),
        out_shape=jax.ShapeDtypeStruct((count, height), jnp.float32),
        in_specs=[
            pl.BlockSpec((count, depth), lambda i: (0, 0)),
            pl.BlockSpec((256, depth), lambda i: (i, 0)),
        ],
        out_specs=pl.BlockSpec((count, 256), lambda i: (0, i)),
        compiler_params=pltpu.CompilerParams(vmem_limit_bytes=16 << 20),
        cost_estimate=pl.CostEstimate(
            flops=2 * count * depth * height,
            bytes_accessed=4 * (count * depth + depth * height + count * height),
            transcendentals=0,
        ),
        name="fit",
    )(rows, transfer)


def adjoint_kernel(rows_ref, tile_ref, out_ref):
    out_ref[...] = jnp.zeros_like(out_ref)

    @pl.loop(0, 2)
    def _(chunk):
        at = pl.multiple_of(chunk * 512, 512)
        out_ref[...] += times(rows_ref[:, pl.ds(at, 512)], tile_ref[pl.ds(at, 512), :], 0)


def adjoint_products(rows, transfer):
    count, depth = rows.shape
    width = transfer.shape[1]
    return pl.pallas_call(
        adjoint_kernel,
        grid=(width // 256,),
        out_shape=jax.ShapeDtypeStruct((count, width), jnp.float32),
        in_specs=[
            pl.BlockSpec((count, depth), lambda i: (0, 0)),
            pl.BlockSpec((depth, 256), lambda i: (0, i)),
        ],
        out_specs=pl.BlockSpec((count, 256), lambda i: (0, i)),
        compiler_params=pltpu.CompilerParams(vmem_limit_bytes=16 << 20),
        cost_estimate=pl.CostEstimate(
            flops=2 * count * depth * width,
            bytes_accessed=4 * (count * depth + depth * width + count * width),
            transcendentals=0,
        ),
        name="adjoint",
    )(rows, transfer)


def fitted_share(blocks, transfer):
    z, xl = lax.axis_index("z"), lax.axis_index("xl")
    made = fit_products(blocks.reshape(256, -1), transfer).reshape(2, 8, 16, -1)

    def pick(side, ahead):
        at = (xl if side == 0 else 1 - xl, (z + ahead + 8) % 8, 0, 0)
        return lax.dynamic_slice(made, at, (1, 1, 16, made.shape[3]))[0, 0]

    distant = across(jnp.concatenate([pick(1, ahead) for ahead in (3, -3, 4)]))
    close = across(jnp.concatenate([pick(1, ahead) for ahead in (2, -2, 1, -1, 0)]))
    up3 = along_z(pick(0, 3) + distant[:16], 1)
    down3 = along_z(pick(0, -3) + distant[16:32], -1)
    up4 = along_z(pick(0, 4) + distant[32:], 2)
    up1 = along_z(pick(0, 1) + close[32:48], 1)
    down1 = along_z(pick(0, -1) + close[48:64], -1)
    up2 = along_z(pick(0, 2) + close[:16] + up3 + up4, 2)
    down2 = along_z(pick(0, -2) + close[16:32] + down3, -2)
    return pick(0, 0) + close[64:] + up1 + down1 + up2 + down2


def adjoint_share(misfit, transfer, share):
    copies = jnp.broadcast_to(misfit[None], (8,) + misfit.shape)
    own = lax.all_to_all(copies, "z", 0, 0, tiled=True).reshape(128, -1)
    other = lax.ppermute(own, "xl", SWAP)
    first_core = lax.axis_index("c") == 0
    lane = lax.broadcasted_iota(jnp.int32, (128, EXT), 1)
    halves = []
    for rows in (own, other):
        squares = jnp.sum(rows * rows, axis=1, keepdims=True)
        made = jnp.concatenate(
            [adjoint_products(rows, transfer), jnp.where(lane < EXT // 2, squares, share)], axis=1
        ).reshape(4, 2, 16, -1)
        mine = jnp.where(first_core, made[:, 0], made[:, 1])
        theirs = jnp.where(first_core, made[:, 1], made[:, 0])
        halves.append(mine + lax.ppermute(theirs, "c", SWAP))
    first = lax.axis_index("xl") == 0
    ordered = jnp.where(first, jnp.concatenate(halves), jnp.concatenate(halves[::-1]))
    parts = lax.all_to_all(ordered.reshape(16, 8, -1), PLANE, 0, 0, tiled=True)
    summed = jnp.sum(parts.reshape(8, 2, 8, -1), axis=0)
    return jnp.concatenate([summed[0], summed[1]], axis=1)


def exchange_z(block):
    return lax.all_to_all(block, "z", 0, 0, tiled=True)


def body(transfer, observed, start, probe, w_first, w_mid, w_last):
    weights = weights_ready(w_first, w_mid, w_last)
    picture = probe.reshape(IMG, IMG).astype(jnp.float32)
    first = lax.axis_index("xl") == 0
    kept = jnp.where(first, start[:8], start[8:])
    moved = lax.ppermute(jnp.where(first, start[8:], start[:8]), "xl", SWAP)
    start_pair = jnp.concatenate(
        [jnp.where(first, kept, moved), jnp.where(first, moved, kept)], axis=1
    )
    share = jnp.sum(transfer * transfer)
    blocks = gather_start(start)
    whole = None
    base = None
    for iteration in range(ITERS):
        misfit = observed - fitted_share(blocks, transfer)
        summed = adjoint_share(misfit, transfer, share)
        last = iteration + 1 == ITERS
        if iteration == 0:
            base = exchange_z(jnp.concatenate([start_pair, summed], axis=1))
            whole = denoise(base, base, 2048, base, picture, weights, last)
        else:
            whole = denoise(whole, exchange_z(summed), 0, base, picture, weights, last)
        if not last:
            blocks = gather_whole(whole)
    return whole


def solution(mesh):
    fine = Mesh(mesh.devices.reshape(2, 4, 2, 2, 8), ROW_AXES + MODE_AXES)
    return jax.shard_map(
        body,
        mesh=fine,
        in_specs=(
            P(ROW_AXES, MODE_AXES),
            P(MODE_AXES, ROW_AXES),
            P(ROW_AXES, MODE_AXES),
            P(ROW_AXES + MODE_AXES, None),
            P(),
            P(),
            P(),
        ),
        out_specs=P(ROW_AXES + MODE_AXES, None),
        check_vma=False,
    )
```
